512 devices in a mesh: pool: 32 (over y, z_lo, core), col: 16 (over x, z_hi).
Axes of the slice: x: 4, y: 4, z: 16 (z_hi: 4, z_lo: 4; z = z_hi * 4 + z_lo), core: 2. Of those that a mesh axis runs over, the one named last changes fastest.
Arguments:
- matrix_elems: bfloat16 [512, 64, 32768], P(None, 'pool', 'col'), may hold values from -6 to 6
- residue: bfloat16 [1024, 32768], P('pool', 'col'), may hold values from -6 to 6
- pole_freq: bfloat16 [1024, 32768], P('pool', 'col'), may hold values from 0.5 to 4
- slab_index: int32 [1024], P('col'), may hold values from 0 to 32767, as said below
- band_order: int32 [64], replicated, may hold values from 0 to 63, each once
- band_mag: float32 [64], replicated, may hold values from 0.1 to 8
Outputs:
- self_energy: float32 [512, 512], P('col')
The draws below stay inside these ranges and needn't reach their ends.
Inputs may be any that keep to these rules, and one draw needn't show every extreme that they name: Block i of slab_index (positions i * 64 to (i + 1) * 64 - 1) holds distinct increasing G-vectors of i * 2048 to (i + 1) * 2048 - 1.
All inputs are finite; a program needn't handle non-finite values.
Results may differ from the reference program's by a relative error of at most 0.004.
Values may be sent and summed in bfloat16 or wider, within the bound.
A program may use at most 128 MiB of HBM per device.

```python
import math
import jax
import jax.numpy as jnp
from jax import lax

NS = 512
NG = 32768
GR = 1024
NBANDS = 64
N_COL = 16


def draw_slab_index(key, part):
    group_width = NG // N_COL
    owned_rows = GR // N_COL
    sub_keys = jax.random.split(key, N_COL)

    def one_owner(sub_key, owner):
        inner = jax.random.permutation(sub_key, group_width - 2)[:owned_rows - 2].astype(jnp.int32) + 1
        offsets = jnp.concatenate([jnp.zeros((1,), jnp.int32), jnp.sort(inner), jnp.full((1,), group_width - 1, jnp.int32)])
        return offsets + owner * group_width
    owners = jnp.arange(N_COL, dtype=jnp.int32)
    return jax.vmap(one_owner)(sub_keys, owners).reshape(-1).astype(jnp.int32)


def with_spikes(drawn, rng, source, target, blocks, factor):
    def block_of(axis_at):
        return (jnp.arange(drawn.shape[axis_at]) // (drawn.shape[axis_at] // blocks)).reshape((-1,) + (1,) * (drawn.ndim - 1 - axis_at))

    first = jax.random.permutation(rng, blocks)[block_of(target)]
    far = (block_of(target) + blocks // 2) % blocks
    return jnp.where((block_of(source) == first) | (block_of(source) == far), factor * drawn, drawn)


def shard_levels(stream_key, extent, cuts, low, largest):
    factor_of, own = 1.0, jax.random.fold_in(stream_key, 6)
    for axis_at, shards_of in cuts:
        steps = jnp.exp(jax.random.uniform(jax.random.fold_in(own, axis_at), (shards_of,), jnp.float32, low / len(cuts), largest / len(cuts)))
        factor_of = factor_of * jnp.repeat(steps, extent[axis_at] // shards_of).reshape([-1 if axis == axis_at else 1 for axis in range(len(extent))])
    return factor_of


def bell_draw(key, dims, scale, bound, shards=(), kind=jnp.bfloat16):
    factor_of = shard_levels(key, dims, shards, -0.22, 0.18) if shards else 1.0
    values = jax.random.normal(key, dims, jnp.float32) * scale * factor_of
    return jnp.minimum(jnp.maximum(values, -bound), bound).astype(kind)


def gaussian_with(own_key, extent, scale, most, cuts, heavy, kind=jnp.bfloat16):
    drawn = scale * jax.random.normal(own_key, extent, jnp.float32)
    if cuts:
        drawn = drawn * shard_levels(own_key, extent, cuts, -0.22, 0.18)
    return jnp.clip(with_spikes(drawn, jax.random.fold_in(own_key, 3), *heavy), -most, most).astype(kind)


def setup_inputs(seed: int = 0) -> dict:
    key_list = jax.random.split(jax.random.key(seed), 7)
    return {
        "matrix_elems": gaussian_with(key_list[0], (NS, NBANDS, NG), 1.0, 6.0, ((1, 32), (2, 16)), (2, 0, 16, 2.0)),
        "residue": bell_draw(key_list[1], (GR, NG), 1.0, 6.0, ((0, 32), (1, 16))),
        "pole_freq": jnp.clip(jnp.exp(math.log(4.0) - 2.0794415 * jax.random.uniform(key_list[2], (GR, NG), jnp.float32) ** shard_levels(key_list[2], (GR, NG), ((0, 32), (1, 16)), -0.2, 0.2)), 0.5, 4.0).astype(jnp.bfloat16),
        "slab_index": draw_slab_index(jax.random.fold_in(key_list[6], 71), 0),
        "band_order": jax.random.permutation(key_list[4], NBANDS).astype(jnp.int32),
        "band_mag": jnp.clip(jnp.exp(jax.random.uniform(key_list[5], (NBANDS,), jnp.float32, math.log(0.1), math.log(8.0))), 0.1, 8.0),
    }


broadening = 0.25

def pole_weights(res_rows, pole_rows, magnitude, parity):
    detuning = pole_rows.astype(jnp.float32)[None] + magnitude[:, None, None]
    signed_gap = parity[:, None, None] * detuning
    scaled = res_rows.astype(jnp.float32)[None] * signed_gap / (signed_gap * signed_gap + broadening * broadening)
    return scaled.astype(jnp.bfloat16)

def reference(matrix_elems, residue, pole_freq, slab_index, band_order, band_mag):
    band_total = band_order.shape[0]
    occupied = band_total // 4
    magnitude = band_mag[band_order]
    parity = jnp.where(band_order < occupied, 1.0, -1.0).astype(jnp.float32)
    slab_elems = jnp.take(matrix_elems, slab_index, axis=2)
    normalizer = 1.0 / jnp.sqrt(jnp.float32(band_total) * residue.shape[0] * residue.shape[1])
    states = matrix_elems.shape[0]

    def accumulate(running, member):
        member_mag = lax.dynamic_slice_in_dim(magnitude, member, 1)
        member_parity = lax.dynamic_slice_in_dim(parity, member, 1)
        weights = pole_weights(residue, pole_freq, member_mag, member_parity)[0]
        left_rows = lax.dynamic_index_in_dim(slab_elems, member, 1, keepdims=False)
        mixed_rows = jnp.dot(left_rows, weights, preferred_element_type=jnp.float32).astype(jnp.bfloat16)
        right_rows = lax.dynamic_index_in_dim(matrix_elems, member, 1, keepdims=False)
        term = lax.dot_general(mixed_rows, right_rows, (((1,), (1,)), ((), ())), preferred_element_type=jnp.float32)
        return (running + term, None)
    running, unused = lax.scan(accumulate, jnp.zeros((states, states), jnp.float32), jnp.arange(band_total, dtype=jnp.int32))
    return running * normalizer
```

```python
import jax
import jax.numpy as jnp
from jax import lax
from jax.experimental import pallas as pl
from jax.experimental.pallas import tpu as pltpu
from jax.sharding import PartitionSpec as P

broadening = 0.25
SIDE = 4


class Place:
    def __init__(self):
        pool, col = lax.axis_index("pool"), lax.axis_index("col")
        self.y, self.z, self.c = pool // 8, (pool // 2) % 4, pool % 2
        self.x, self.h = col // 4, col % 4

    def at(self, **moved):
        y, z, c, x, h = (moved.get(k, getattr(self, k)) for k in "yzcxh")
        return ((y * 4 + z) * 2 + c, x * 4 + h)


def ring(at, by):
    return lax.rem(at + by + SIDE, SIDE)


class Sends:
    def __init__(self, sems):
        self.sems, self.count, self.kept = sems, 0, []

    def start(self, src, dst, recv_sem, device, when=None):
        slot = self.count
        self.count += 1

        def made():
            return pltpu.make_async_remote_copy(
                src_ref=src(), dst_ref=dst(), send_sem=self.sems.at[slot], recv_sem=recv_sem(),
                device_id=device, device_id_type=pl.DeviceIdType.MESH)

        if when is None:
            made().start()
        else:
            pl.when(when)(lambda: made().start())
        self.kept.append((made, when))

    def finish(self):
        for made, when in self.kept:
            if when is None:
                made().wait_send()
            else:
                pl.when(when)(lambda made=made: made().wait_send())


def arrived(view, sem, device):
    pltpu.make_async_remote_copy(
        src_ref=view, dst_ref=view, send_sem=sem, recv_sem=sem,
        device_id=device, device_id_type=pl.DeviceIdType.MESH).wait_recv()


def greet(devices):
    barrier = pltpu.get_barrier_semaphore()
    total = jnp.int32(0)
    for device, when in devices:
        def signal(device=device):
            pl.semaphore_signal(
                barrier, inc=1, device_id=device, device_id_type=pl.DeviceIdType.MESH)
        if when is None:
            signal()
            total = total + 1
        else:
            pl.when(when)(signal)
            total = total + when.astype(jnp.int32)
    pl.semaphore_wait(barrier, total)


def gather_partners(me):
    pairs = [(me.at(c=1 - me.c), None)]
    for by in (1, -1):
        pairs += [(me.at(y=ring(me.y, by)), None), (me.at(x=ring(me.x, by)), None),
                  (me.at(h=ring(me.h, by)), None)]
    pairs += [(me.at(z=me.z + 1), me.z < 3), (me.at(z=me.z - 1), me.z > 0)]
    return pairs


def gather_steps(me, sends, own, full, pick, slab, pole_sems, twin_sems, slab_sems):
    rows, depth = own[0].shape[0], pick.shape[1]

    def pole_view(half, y, z, c):
        at = ((y * 4 + z) * 2 + c) * rows
        return full[half].at[pl.ds(pl.multiple_of(at, rows), rows)]

    def pole_source(half, y, z, mine):
        return own[half] if mine else pole_view(half, y, z, me.c)

    def send_pole(half, y, z, device, when=None, mine=False):
        sends.start(lambda: pole_source(half, y, z, mine), lambda: pole_view(half, y, z, me.c),
                    lambda: pole_sems.at[(y * 4 + z) * 2 + half], device, when)

    def send_twin(half, y, z, when=None, mine=False):
        sends.start(lambda: pole_source(half, y, z, mine), lambda: pole_view(half, y, z, me.c),
                    lambda: twin_sems.at[(y * 4 + z) * 2 + half], me.at(c=1 - me.c), when)

    def await_pole(half, y, z, when=None):
        def waits():
            arrived(pole_view(half, y, z, me.c), pole_sems.at[(y * 4 + z) * 2 + half], me.at(c=1 - me.c))
        waits() if when is None else pl.when(when)(waits)

    def await_twin(half, y, z):
        arrived(pole_view(half, y, z, 1 - me.c), twin_sems.at[(y * 4 + z) * 2 + half], me.at(c=1 - me.c))

    def slab_view(half, x, h):
        return slab.at[half, pl.ds(pl.multiple_of((x * 4 + h) * depth, depth), depth)]

    def send_slab(half, x, h, device, mine=False):
        sends.start(lambda: pick.at[half] if mine else slab_view(half, x, h),
                    lambda: slab_view(half, x, h), lambda: slab_sems.at[(x * 4 + h) * 2 + half], device)

    def await_slab(half, x, h):
        arrived(slab_view(half, x, h), slab_sems.at[(x * 4 + h) * 2 + half], me.at(c=1 - me.c))

    up, down = me.at(y=ring(me.y, 1)), me.at(y=ring(me.y, -1))
    east, west = me.at(x=ring(me.x, 1)), me.at(x=ring(me.x, -1))
    far, near = me.at(h=ring(me.h, 1)), me.at(h=ring(me.h, -1))
    right, left = me.at(z=me.z + 1), me.at(z=me.z - 1)

    def along_y(z, when=None, mine=False):
        for half in (0, 1):
            send_pole(half, me.y, z, up, when, mine)
            send_pole(half, me.y, z, down, when, mine)

    def to_twin(y, z, when=None, mine=False):
        for half in (0, 1):
            send_twin(half, y, z, when, mine)

    def from_y(z, when=None):
        below, above = ring(me.y, -1), ring(me.y, 1)
        await_pole(0, below, z, when)
        send_pole(0, below, z, up, when)
        await_pole(1, above, z, when)
        send_pole(1, above, z, down, when)
        await_pole(1, below, z, when)
        await_pole(0, above, z, when)
        to_twin(below, z, when)
        to_twin(above, z, when)

    def from_opposite(z, when=None):
        across = ring(me.y, 2)
        for half in (0, 1):
            await_pole(half, across, z, when)
            send_twin(half, across, z, when)

    def from_z(by):
        for sign, onward, can in ((-1, right, me.z < 3), (1, left, me.z > 0)):
            z = me.z + sign * by
            there = (z >= 0) & (z <= 3)
            for half in (0, 1):
                await_pole(half, me.y, z, there)
                if by < 3:
                    send_pole(half, me.y, z, onward, there & can)
            along_y(z, there)
            to_twin(me.y, z, there)

    def sources(by):
        return [(z, (z >= 0) & (z <= 3)) for z in (me.z - by, me.z + by)]

    def along_x(h, mine=False):
        for half in (0, 1):
            send_slab(half, me.x, h, east, mine)
            send_slab(half, me.x, h, west, mine)

    def from_x(h):
        behind, ahead = ring(me.x, -1), ring(me.x, 1)
        await_slab(0, behind, h)
        send_slab(0, behind, h, east)
        await_slab(1, ahead, h)
        send_slab(1, ahead, h, west)
        await_slab(1, behind, h)
        await_slab(0, ahead, h)

    def from_x_opposite(h):
        for half in (0, 1):
            await_slab(half, ring(me.x, 2), h)

    behind, ahead, across = ring(me.h, -1), ring(me.h, 1), ring(me.h, 2)

    def first():
        for half in (0, 1):
            send_pole(half, me.y, me.z, right, me.z < 3, True)
            send_pole(half, me.y, me.z, left, me.z > 0, True)
        along_y(me.z, None, True)
        to_twin(me.y, me.z, None, True)

    def slab_first():
        for half in (0, 1):
            send_slab(half, me.x, me.h, far, True)
            send_slab(half, me.x, me.h, near, True)
        along_x(me.h, True)

    def slab_second():
        await_slab(0, me.x, behind)
        send_slab(0, me.x, behind, far)
        await_slab(1, me.x, ahead)
        send_slab(1, me.x, ahead, near)
        await_slab(1, me.x, behind)
        await_slab(0, me.x, ahead)
        along_x(behind)
        along_x(ahead)

    def slab_third():
        for half in (0, 1):
            await_slab(half, me.x, across)
        along_x(across)

    def rest():
        from_z(1)
        from_y(me.z)
        slab_second()
        from_x(me.h)
        from_z(2)
        from_opposite(me.z)
        for z, there in sources(1):
            from_y(z, there)
        from_z(3)
        slab_third()
        from_x(behind)
        from_x(ahead)
        from_x_opposite(me.h)
        for z, there in sources(1):
            from_opposite(z, there)
        for z, there in sources(2):
            from_y(z, there)
        from_x(across)
        for h in (behind, ahead, across):
            from_x_opposite(h)
        for z, there in sources(3):
            from_y(z, there)
        for by in (2, 3):
            for z, there in sources(by):
                from_opposite(z, there)
        for y in range(SIDE):
            for z in range(SIDE):
                for half in (0, 1):
                    await_twin(half, y, z)

    return first, slab_first, rest


GATHER_SENDS = 220


def gather_kernel(pole, res, pick, poles, ress, slab, send_sems, pole_sems, twin_sems, slab_sems, own_sem):
    me = Place()
    rows, depth = pole.shape[0], pick.shape[1]
    greet(gather_partners(me))
    sends = Sends(send_sems)
    first, slab_first, rest = gather_steps(
        me, sends, (pole, res), (poles, ress), pick, slab, pole_sems, twin_sems, slab_sems)
    first()
    slab_first()
    at = pl.multiple_of(((me.y * 4 + me.z) * 2 + me.c) * rows, rows)
    poles[pl.ds(at, rows)] = pole[...]
    ress[pl.ds(at, rows)] = res[...]
    for half in (0, 1):
        slab[half, pl.ds(pl.multiple_of((me.x * 4 + me.h) * depth, depth), depth)] = pick[half]
    rest()
    sends.finish()


def gathered(pole, res, pick):
    dma = pltpu.SemaphoreType.DMA
    vmem = pl.BlockSpec(memory_space=pltpu.VMEM)
    rows, width = pole.shape
    return pl.pallas_call(
        gather_kernel,
        out_shape=(
            jax.ShapeDtypeStruct((rows * 32, width), pole.dtype),
            jax.ShapeDtypeStruct((rows * 32, width), res.dtype),
            jax.ShapeDtypeStruct((2, pick.shape[1] * 16, pick.shape[2]), pick.dtype),
        ),
        in_specs=[vmem] * 3,
        out_specs=(vmem,) * 3,
        scratch_shapes=[dma((GATHER_SENDS,)), dma((32,)), dma((32,)), dma((32,)), dma((1,))],
        compiler_params=pltpu.CompilerParams(
            collective_id=0, has_side_effects=True, vmem_limit_bytes=48 * 2**20),
    )(pole, res, pick)


def reduce_partners(me):
    pairs = [(me.at(c=1 - me.c), None)]
    for by in (1, 2, 3):
        y = ring(me.y, by)
        pairs += [(me.at(x=ring(me.x, by)), None), (me.at(h=ring(me.h, by)), None),
                  (me.at(z=ring(me.z, by)), None), (me.at(y=y), None), (me.at(y=y, c=1 - me.c), None)]
    return pairs


REDUCE_SENDS = 20


def reduce_steps(me, sends, part, out, mine, twin, x_in, x_sum, y_in, y_sum, h_in, z_all, last, sems):
    other = me.at(c=1 - me.c)

    def await_(view, slot):
        arrived(view, sems.at[slot], other)

    def send(src, dst, slot, device):
        sends.start(lambda: src, lambda: dst, lambda: sems.at[slot], device)

    width = mine.shape[-1]
    theirs = pl.ds(pl.multiple_of((1 - me.c) * width, width), width)
    ours = pl.ds(pl.multiple_of(me.c * width, width), width)
    for by in (1, 2, 3, 0):
        x = ring(me.x, by)
        block = pl.ds(pl.multiple_of(x * 128, 128), 128)
        send(part.at[block, theirs], twin.at[x], by, other)
    for by in (1, 2, 3, 0):
        x = ring(me.x, by)
        block = pl.ds(pl.multiple_of(x * 128, 128), 128)
        await_(twin.at[x], by)
        summed = part[block, ours] + twin[x]
        if by:
            mine[x] = summed
            send(mine.at[x], x_in.at[by - 1], 4 + by - 1, me.at(x=x))
        else:
            x_sum[...] = summed.reshape(x_sum.shape)
    total = x_sum[...]
    for by in (3, 1, 2):
        await_(x_in.at[by - 1], 4 + by - 1)
        total = total + x_in[by - 1].reshape(x_sum.shape)
    x_sum[...] = total
    for by in (2, 1, 3):
        y = ring(me.y, by)
        send(x_sum.at[:, y], y_in.at[by - 1], 7 + by - 1, me.at(y=y))
    total = x_sum[:, me.y]
    for by in (3, 1, 2):
        await_(y_in.at[by - 1], 7 + by - 1)
        total = total + y_in[by - 1]
    y_sum[...] = total
    for by in (2, 1, 3):
        h = ring(me.h, by)
        send(y_sum.at[h], h_in.at[by - 1], 10 + by - 1, me.at(h=h))
    total = y_sum[me.h]
    for by in (3, 1, 2):
        await_(h_in.at[by - 1], 10 + by - 1)
        total = total + h_in[by - 1]
    z_all[me.z] = total
    for by in (2, 1, 3):
        z = ring(me.z, by)
        send(z_all.at[me.z], z_all.at[me.z], 13 + me.z, me.at(z=z))
    for by in (3, 1, 2):
        z = ring(me.z, by)
        await_(z_all.at[z], 13 + z)
    last[...] = (z_all[0] + z_all[1]) + (z_all[2] + z_all[3])
    rows = pl.ds(pl.multiple_of(me.y * 8, 8), 8)
    slot = 17 + me.y * 2 + me.c
    for by in (2, 1, 3):
        y = ring(me.y, by)
        send(last, out.at[rows, ours], slot, me.at(y=y))
        send(last, out.at[rows, ours], slot, me.at(y=y, c=1 - me.c))
    send(last, out.at[rows, ours], slot, other)
    out[rows, ours] = last[...]
    for by in (0, 1, 2, 3):
        y = ring(me.y, by)
        there = pl.ds(pl.multiple_of(y * 8, 8), 8)
        if by:
            await_(out.at[there, ours], 17 + y * 2 + me.c)
        await_(out.at[there, theirs], 17 + y * 2 + 1 - me.c)


def reduce_scratch():
    f32 = jnp.float32
    return [
        pltpu.VMEM((4, 128, 256), f32), pltpu.VMEM((4, 128, 256), f32),
        pltpu.VMEM((3, 128, 256), f32), pltpu.VMEM((4, 4, 8, 256), f32),
        pltpu.VMEM((3, 4, 8, 256), f32), pltpu.VMEM((4, 8, 256), f32),
        pltpu.VMEM((3, 8, 256), f32), pltpu.VMEM((4, 8, 256), f32),
        pltpu.VMEM((8, 256), f32), pltpu.SemaphoreType.DMA((25,)),
    ]


def reduce_kernel(part, out, send_sems, *scratch):
    me = Place()
    greet(reduce_partners(me))
    sends = Sends(send_sems)
    reduce_steps(me, sends, part, out, *scratch)
    sends.finish()


def reduced(part):
    vmem = pl.BlockSpec(memory_space=pltpu.VMEM)
    return pl.pallas_call(
        reduce_kernel,
        out_shape=jax.ShapeDtypeStruct((32, part.shape[1]), jnp.float32),
        in_specs=[vmem],
        out_specs=vmem,
        scratch_shapes=[pltpu.SemaphoreType.DMA((32,))] + reduce_scratch(),
        compiler_params=pltpu.CompilerParams(collective_id=1, has_side_effects=True),
    )(part)


def pole_weights(res_rows, pole_rows, magnitude, parity):
    detuning = pole_rows.astype(jnp.float32)[None] + magnitude[:, None, None]
    signed_gap = parity[:, None, None] * detuning
    scaled = (
        res_rows.astype(jnp.float32)[None]
        * signed_gap
        / (signed_gap * signed_gap + broadening * broadening)
    )
    return scaled.astype(jnp.bfloat16)


def on_device(matrix_elems, residue, pole_freq, slab_index, band_order, band_mag):
    pool_at = lax.axis_index("pool")
    col_at = lax.axis_index("col")
    band_total = band_order.shape[0]
    occupied = band_total // 4
    members = matrix_elems.shape[1]
    column_count = matrix_elems.shape[2]
    slab_total = residue.shape[0] * lax.axis_size("pool")
    ordinals = lax.dynamic_slice_in_dim(band_order, pool_at * members, members)
    matches = ordinals[:, None] == jnp.arange(band_total, dtype=jnp.int32)[None, :]
    magnitude = jnp.sum(jnp.where(matches, band_mag[None, :], 0.0), axis=1)
    parity = jnp.where(ordinals < occupied, 1.0, -1.0).astype(jnp.float32)
    local_rows = slab_index - col_at * column_count
    chosen = (local_rows[:, None] == jnp.arange(column_count, dtype=jnp.int32)[None, :]).astype(jnp.bfloat16)
    picked = jnp.einsum(
        "rg,njg->jrn", chosen, matrix_elems, preferred_element_type=jnp.float32
    ).astype(jnp.bfloat16)
    poles, residues, slab_elems = gathered(pole_freq, residue, picked)
    weights = pole_weights(residues, poles, magnitude, parity)
    mixed_rows = jnp.einsum(
        "jrn,jrg->jng", slab_elems, weights, preferred_element_type=jnp.float32
    ).astype(jnp.bfloat16)
    normalizer = 1.0 / jnp.sqrt(
        jnp.float32(band_total) * slab_total * column_count * lax.axis_size("col"))
    part = jnp.einsum(
        "jng,mjg->nm", mixed_rows, matrix_elems, preferred_element_type=jnp.float32)
    return reduced(part * normalizer)


def solution(mesh):
    placed = (P(None, "pool", "col"), P("pool", "col"), P("pool", "col"), P("col"), P(), P())
    return jax.shard_map(
        on_device, mesh=mesh, in_specs=placed, out_specs=P("col", None), check_vma=False
    )
```

```python
import functools

import jax
import jax.numpy as jnp
import numpy as np
from jax import lax
from jax.experimental import pallas as pl
from jax.experimental.pallas import tpu as pltpu
from jax.sharding import PartitionSpec as P

broadening = 0.25
SIDE = 4
SENDS = 200


class Place:
    def __init__(self):
        pool, col = lax.axis_index("pool"), lax.axis_index("col")
        self.y, self.z, self.c = pool // 8, (pool // 2) % 4, pool % 2
        self.x, self.h = col // 4, col % 4

    def at(self, **moved):
        y, z, c, x, h = (moved.get(k, getattr(self, k)) for k in "yzcxh")
        return ((y * 4 + z) * 2 + c, x * 4 + h)


def ring(at, by):
    return lax.rem(at + by + SIDE, SIDE)


class Sends:
    def __init__(self, sems):
        self.sems, self.count, self.kept = sems, 0, []

    def start(self, src, dst, recv_sem, device, when=None):
        slot = self.count
        self.count += 1

        def made():
            return pltpu.make_async_remote_copy(
                src_ref=src(), dst_ref=dst(), send_sem=self.sems.at[slot], recv_sem=recv_sem(),
                device_id=device, device_id_type=pl.DeviceIdType.MESH)

        if when is None:
            made().start()
        else:
            pl.when(when)(lambda: made().start())
        self.kept.append((made, when))

    def finish(self):
        for made, when in self.kept:
            if when is None:
                made().wait_send()
            else:
                pl.when(when)(lambda made=made: made().wait_send())


def arrived(view, sem, device):
    pltpu.make_async_remote_copy(
        src_ref=view, dst_ref=view, send_sem=sem, recv_sem=sem,
        device_id=device, device_id_type=pl.DeviceIdType.MESH).wait_recv()


def greet(devices):
    barrier = pltpu.get_barrier_semaphore()
    total = jnp.int32(0)
    for device, when in devices:
        def signal(device=device):
            pl.semaphore_signal(
                barrier, inc=1, device_id=device, device_id_type=pl.DeviceIdType.MESH)
        if when is None:
            signal()
            total = total + 1
        else:
            pl.when(when)(signal)
            total = total + when.astype(jnp.int32)
    pl.semaphore_wait(barrier, total)


def gather_partners(me):
    pairs = [(me.at(c=1 - me.c), None)]
    for by in (1, -1):
        pairs += [(me.at(y=ring(me.y, by)), None), (me.at(x=ring(me.x, by)), None),
                  (me.at(h=ring(me.h, by)), None)]
    pairs += [(me.at(z=me.z + 1), me.z < 3), (me.at(z=me.z - 1), me.z > 0)]
    return pairs


def gather_steps(me, sends, full, slab, pole_sems, twin_sems, slab_sems, weigh):
    rows, depth = full[0].shape[0] // 32, slab.shape[1] // 16
    twin = me.at(c=1 - me.c)
    pending = []

    def pole_view(half, y, z, c):
        at = ((y * 4 + z) * 2 + c) * rows
        return full[half].at[pl.ds(pl.multiple_of(at, rows), rows)]

    def send_pole(half, y, z, device, when=None):
        sends.start(lambda: pole_view(half, y, z, me.c), lambda: pole_view(half, y, z, me.c),
                    lambda: pole_sems.at[(y * 4 + z) * 2 + half], device, when)

    def send_twin(half, y, z, when=None):
        sends.start(lambda: pole_view(half, y, z, me.c), lambda: pole_view(half, y, z, me.c),
                    lambda: twin_sems.at[(y * 4 + z) * 2 + half], twin, when)

    def await_pole(half, y, z, when=None):
        def waits():
            arrived(pole_view(half, y, z, me.c), pole_sems.at[(y * 4 + z) * 2 + half], twin)
        waits() if when is None else pl.when(when)(waits)

    def slab_view(half, x, h):
        return slab.at[half, pl.ds(pl.multiple_of((x * 4 + h) * depth, depth), depth)]

    def send_slab(half, x, h, device):
        sends.start(lambda: slab_view(half, x, h), lambda: slab_view(half, x, h),
                    lambda: slab_sems.at[(x * 4 + h) * 2 + half], device)

    def await_slab(half, x, h):
        arrived(slab_view(half, x, h), slab_sems.at[(x * 4 + h) * 2 + half], twin)

    up, down = me.at(y=ring(me.y, 1)), me.at(y=ring(me.y, -1))
    east, west = me.at(x=ring(me.x, 1)), me.at(x=ring(me.x, -1))
    far, near = me.at(h=ring(me.h, 1)), me.at(h=ring(me.h, -1))
    right, left = me.at(z=me.z + 1), me.at(z=me.z - 1)

    def drain(count=None):
        for y, z, when in pending[:count]:
            def waits_and_weighs(y=y, z=z):
                for half in (0, 1):
                    arrived(pole_view(half, y, z, 1 - me.c), twin_sems.at[(y * 4 + z) * 2 + half], twin)
                weigh(y, z)
            waits_and_weighs() if when is None else pl.when(when)(waits_and_weighs)
        del pending[:count]

    def along_y(z, when=None):
        for half in (0, 1):
            send_pole(half, me.y, z, up, when)
            send_pole(half, me.y, z, down, when)

    def to_twin(y, z, when=None):
        for half in (0, 1):
            send_twin(half, y, z, when)
        pending.append((y, z, when))

    def from_y(z, when=None):
        below, above = ring(me.y, -1), ring(me.y, 1)
        await_pole(0, below, z, when)
        send_pole(0, below, z, up, when)
        await_pole(1, above, z, when)
        send_pole(1, above, z, down, when)
        await_pole(1, below, z, when)
        await_pole(0, above, z, when)
        to_twin(below, z, when)
        to_twin(above, z, when)

    def from_opposite(z, when=None):
        across = ring(me.y, 2)
        for half in (0, 1):
            await_pole(half, across, z, when)
        to_twin(across, z, when)

    def from_z(by):
        for sign, onward, can in ((-1, right, me.z < 3), (1, left, me.z > 0)):
            z = me.z + sign * by
            there = (z >= 0) & (z <= 3)
            for half in (0, 1):
                await_pole(half, me.y, z, there)
                if by < 3:
                    send_pole(half, me.y, z, onward, there & can)
            along_y(z, there)
            to_twin(me.y, z, there)

    def sources(by):
        return [(z, (z >= 0) & (z <= 3)) for z in (me.z - by, me.z + by)]

    def along_x(h):
        for half in (0, 1):
            send_slab(half, me.x, h, east)
            send_slab(half, me.x, h, west)

    def from_x(h):
        behind, ahead = ring(me.x, -1), ring(me.x, 1)
        await_slab(0, behind, h)
        send_slab(0, behind, h, east)
        await_slab(1, ahead, h)
        send_slab(1, ahead, h, west)
        await_slab(1, behind, h)
        await_slab(0, ahead, h)

    def from_x_opposite(h):
        for half in (0, 1):
            await_slab(half, ring(me.x, 2), h)

    behind, ahead, across = ring(me.h, -1), ring(me.h, 1), ring(me.h, 2)

    def first():
        for half in (0, 1):
            send_pole(half, me.y, me.z, right, me.z < 3)
            send_pole(half, me.y, me.z, left, me.z > 0)
        along_y(me.z)
        to_twin(me.y, me.z)

    def slab_first():
        for half in (0, 1):
            send_slab(half, me.x, me.h, far)
            send_slab(half, me.x, me.h, near)
        along_x(me.h)

    def slab_second():
        await_slab(0, me.x, behind)
        send_slab(0, me.x, behind, far)
        await_slab(1, me.x, ahead)
        send_slab(1, me.x, ahead, near)
        await_slab(1, me.x, behind)
        await_slab(0, me.x, ahead)
        along_x(behind)
        along_x(ahead)

    def slab_third():
        for half in (0, 1):
            await_slab(half, me.x, across)
        along_x(across)

    def rest():
        from_z(1)
        slab_first()
        drain(1)
        from_z(2)
        from_y(me.z)
        drain(2)
        from_z(3)
        for z, there in sources(1):
            from_y(z, there)
        from_opposite(me.z)
        slab_second()
        drain(4)
        for z, there in sources(2):
            from_y(z, there)
        from_x(me.h)
        drain(4)
        for z, there in sources(1):
            from_opposite(z, there)
        slab_third()
        from_x(behind)
        from_x(ahead)
        drain(5)
        for z, there in sources(3):
            from_y(z, there)
        for z, there in sources(2):
            from_opposite(z, there)
        from_x(across)
        drain(len(pending) - 3)
        for h in (me.h, behind, ahead, across):
            from_x_opposite(h)

    def last():
        for z, there in sources(3):
            from_opposite(z, there)
        drain()

    return first, rest, last


def far_partners(me):
    pairs = [(me.at(x=ring(me.x, 2)), None), (me.at(h=ring(me.h, 2)), None), (me.at(y=ring(me.y, 2)), None)]
    for by in (1, 2, 3):
        pairs += [(me.at(y=ring(me.y, by), c=1 - me.c), None)]
        z = ring(me.z, by)
        pairs += [(me.at(z=z), jnp.abs(z - me.z) > 1)]
    return pairs


def reduce_steps(me, sends, part, out, out_twin, mine, twin, x_in, x_sum, y_in, y_sum, h_in, z_all, last, sems):
    other = me.at(c=1 - me.c)

    def await_(view, slot):
        arrived(view, sems.at[slot], other)

    def send(src, dst, slot, device):
        sends.start(lambda: src, lambda: dst, lambda: sems.at[slot], device)

    width = mine.shape[-1]
    theirs = pl.ds(pl.multiple_of((1 - me.c) * width, width), width)
    ours = pl.ds(pl.multiple_of(me.c * width, width), width)
    for by in (2, 1, 3, 0):
        x = ring(me.x, by)
        block = pl.ds(pl.multiple_of(x * 128, 128), 128)
        out_twin[x] = part[block, theirs].astype(jnp.bfloat16)
        send(out_twin.at[x], twin.at[x], by, other)
    for by in (2, 1, 3, 0):
        x = ring(me.x, by)
        block = pl.ds(pl.multiple_of(x * 128, 128), 128)
        await_(twin.at[x], by)
        summed = part[block, ours] + twin[x].astype(jnp.float32)
        if by:
            mine[x] = summed.astype(jnp.bfloat16)
            send(mine.at[x], x_in.at[by - 1], 4 + by - 1, me.at(x=x))
        else:
            x_sum[...] = summed.reshape(x_sum.shape)
    total = x_sum[...]
    for by in (3, 1, 2):
        await_(x_in.at[by - 1], 4 + by - 1)
        total = total + x_in[by - 1].astype(jnp.float32).reshape(x_sum.shape)
    x_sum[...] = total
    for by in (2, 1, 3):
        y = ring(me.y, by)
        send(x_sum.at[:, y], y_in.at[by - 1], 7 + by - 1, me.at(y=y))
    total = x_sum[:, me.y]
    for by in (3, 1, 2):
        await_(y_in.at[by - 1], 7 + by - 1)
        total = total + y_in[by - 1]
    y_sum[...] = total
    for by in (2, 1, 3):
        h = ring(me.h, by)
        send(y_sum.at[h], h_in.at[by - 1], 10 + by - 1, me.at(h=h))
    total = y_sum[me.h]
    for by in (3, 1, 2):
        await_(h_in.at[by - 1], 10 + by - 1)
        total = total + h_in[by - 1]
    z_all[me.z] = total
    for by in (2, 1, 3):
        z = ring(me.z, by)
        send(z_all.at[me.z], z_all.at[me.z], 13 + me.z, me.at(z=z))
    for by in (3, 1, 2):
        z = ring(me.z, by)
        await_(z_all.at[z], 13 + z)
    last[...] = (z_all[0] + z_all[1]) + (z_all[2] + z_all[3])
    rows = pl.ds(pl.multiple_of(me.y * 8, 8), 8)
    slot = 17 + me.y * 2 + me.c
    for by in (2, 1, 3):
        y = ring(me.y, by)
        send(last, out.at[rows, ours], slot, me.at(y=y))
        send(last, out.at[rows, ours], slot, me.at(y=y, c=1 - me.c))
    send(last, out.at[rows, ours], slot, other)
    out[rows, ours] = last[...]
    for by in (0, 1, 2, 3):
        y = ring(me.y, by)
        there = pl.ds(pl.multiple_of(y * 8, 8), 8)
        if by:
            await_(out.at[there, ours], 17 + y * 2 + me.c)
        await_(out.at[there, theirs], 17 + y * 2 + 1 - me.c)


def reduce_scratch():
    f32, bf16 = jnp.float32, jnp.bfloat16
    return [
        pltpu.VMEM((4, 128, 256), bf16), pltpu.VMEM((4, 128, 256), bf16),
        pltpu.VMEM((4, 128, 256), bf16), pltpu.VMEM((3, 128, 256), bf16),
        pltpu.VMEM((4, 4, 8, 256), f32),
        pltpu.VMEM((3, 4, 8, 256), f32), pltpu.VMEM((4, 8, 256), f32),
        pltpu.VMEM((3, 8, 256), f32), pltpu.VMEM((4, 8, 256), f32),
        pltpu.VMEM((8, 256), f32), pltpu.SemaphoreType.DMA((25,)),
    ]


def chosen_band(order, mags, slot, occupied):
    lanes = lax.broadcasted_iota(jnp.int32, order.shape, 1)
    band = jnp.sum(jnp.where(lanes == slot, order, 0), axis=1, keepdims=True)
    magnitude = jnp.sum(jnp.where(lanes == band, mags, 0.0), axis=1, keepdims=True)
    return magnitude, jnp.where(band < occupied, 1.0, -1.0).astype(jnp.float32)


def whole_kernel(normalizer, elems_hbm, res_hbm, pole_hbm, index, order, mags, out,
                 elems, split, poles, ress, slab, slab_n, weights, part,
                 send_sems, pole_sems, twin_sems, slab_sems, own_sems, *reduce_refs):
    me = Place()
    rows, width = pole_hbm.shape
    states = elems.shape[0]
    depth = index.shape[1]
    pool, col = lax.axis_index("pool"), lax.axis_index("col")
    bf16, f32 = jnp.bfloat16, jnp.float32
    at = pl.ds(pl.multiple_of(pool * rows, rows), rows)
    loads = [
        pltpu.make_async_copy(pole_hbm, poles.at[at], own_sems.at[0]),
        pltpu.make_async_copy(res_hbm, ress.at[at], own_sems.at[1]),
        pltpu.make_async_copy(elems_hbm, elems, own_sems.at[2]),
    ]
    for load in loads:
        load.start()
    greet(gather_partners(me) + far_partners(me))
    sends = Sends(send_sems)
    bands = [chosen_band(order[...], mags[...], pool * 2 + j, order.shape[1] // 4) for j in (0, 1)]

    def weigh(y, z):
        first_row = pl.multiple_of((y * 4 + z) * 2 * rows, 2 * rows)

        def chunk(k, carry):
            here = pl.ds(first_row, 2 * rows), pl.ds(pl.multiple_of(k * 256, 256), 256)
            pole, res = poles[here].astype(f32), ress[here].astype(f32)
            for j, (magnitude, parity) in enumerate(bands):
                gap = parity * (pole + magnitude)
                scaled = res * gap / (gap * gap + broadening * broadening)
                weights[(j,) + here] = scaled.astype(bf16)
            return carry

        lax.fori_loop(0, width // 256, chunk, 0)

    first, rest, last = gather_steps(
        me, sends, (poles, ress), slab, pole_sems, twin_sems, slab_sems, weigh)
    loads[0].wait()
    loads[1].wait()
    first()

    loads[2].wait()
    to = lax.broadcasted_iota(jnp.int32, (256, 256), 0)
    came = lax.broadcasted_iota(jnp.int32, (256, 256), 1)
    swap = (came == (to % 128) * 2 + to // 128).astype(bf16)

    def part_by_slot(i, carry):
        n = pl.ds(pl.multiple_of(i * 128, 128), 128)
        pairs = elems[n].reshape(256, width)
        sorted_rows = jnp.dot(swap, pairs, preferred_element_type=f32).astype(bf16)
        split[0, n] = sorted_rows[:128]
        split[1, n] = sorted_rows[128:]
        return carry

    lax.fori_loop(0, states // 128, part_by_slot, 0)
    diagonal = lax.broadcasted_iota(jnp.int32, (depth, depth), 0) == lax.broadcasted_iota(
        jnp.int32, (depth, depth), 1)
    local = jnp.sum(jnp.where(diagonal, index[...] - col * width, 0), axis=1, keepdims=True)
    chosen = (lax.broadcasted_iota(jnp.int32, (depth, width), 1) == local).astype(bf16)
    own_slab = pl.ds(pl.multiple_of(col * depth, depth), depth)
    for j in (0, 1):
        slab[j, own_slab] = lax.dot_general(
            chosen, split[j], (((1,), (1,)), ((), ())), preferred_element_type=f32).astype(bf16)

    rest()
    for j in (0, 1):
        slab_n[j] = slab[j].T
    last()

    half = states // 2
    for top in (0, half):
        def chunk(k, carry):
            here = pl.ds(pl.multiple_of(k * 256, 256), 256)
            total = None
            for j in (0, 1):
                mixed = jnp.dot(slab_n[j, top:top + half], weights[j, :, here],
                                preferred_element_type=f32).astype(bf16)
                term = lax.dot_general(mixed, split[j, :, here], (((1,), (1,)), ((), ())),
                                       preferred_element_type=f32)
                total = term if total is None else total + term
            part[top:top + half] += total
            return carry

        part[top:top + half] = jnp.zeros((half, states), f32)
        lax.fori_loop(0, width // 256, chunk, 0)
    part[...] = part[...] * normalizer
    reduce_steps(me, sends, part, out, *reduce_refs)
    sends.finish()


def on_device(matrix_elems, residue, pole_freq, slab_index, band_order, band_mag):
    states, members, width = matrix_elems.shape
    rows, slab_rows = residue.shape[0], residue.shape[0] * 32
    bands = band_order.shape[0]
    normalizer = float(1.0 / np.sqrt(np.float32(bands * slab_rows * width * 16)))
    dma, vmem, anywhere = pltpu.SemaphoreType.DMA, pltpu.VMEM, pl.BlockSpec(memory_space=pl.ANY)
    whole = pl.BlockSpec(memory_space=pltpu.VMEM)
    bf16 = jnp.bfloat16
    return pl.pallas_call(
        functools.partial(whole_kernel, normalizer),
        out_shape=jax.ShapeDtypeStruct((states // 16, states), jnp.float32),
        in_specs=[anywhere] * 3 + [whole] * 3,
        out_specs=whole,
        scratch_shapes=[
            vmem((states, members, width), bf16), vmem((members, states, width), bf16),
            vmem((slab_rows, width), bf16), vmem((slab_rows, width), bf16),
            vmem((members, slab_rows, states), bf16), vmem((members, states, slab_rows), bf16),
            vmem((members, slab_rows, width), bf16), vmem((states, states), jnp.float32),
            dma((SENDS,)), dma((32,)), dma((32,)), dma((32,)), dma((3,)),
        ] + reduce_scratch(),
        compiler_params=pltpu.CompilerParams(
            collective_id=0, has_side_effects=True, vmem_limit_bytes=60 * 2**20),
    )(matrix_elems, residue, pole_freq, slab_index[None], band_order[None], band_mag[None])


def solution(mesh):
    placed = (P(None, "pool", "col"), P("pool", "col"), P("pool", "col"), P("col"), P(), P())
    return jax.shard_map(
        on_device, mesh=mesh, in_specs=placed, out_specs=P("col", None), check_vma=False
    )
```

```python
import functools

import jax
import jax.numpy as jnp
import numpy as np
from jax import lax
from jax.experimental import pallas as pl
from jax.experimental.pallas import tpu as pltpu
from jax.sharding import PartitionSpec as P

broadening = 0.25
SIDE = 4
SENDS = 200


class Place:
    def __init__(self):
        pool, col = lax.axis_index("pool"), lax.axis_index("col")
        self.y, self.z, self.c = pool // 8, (pool // 2) % 4, pool % 2
        self.x, self.h = col // 4, col % 4

    def at(self, **moved):
        y, z, c, x, h = (moved.get(k, getattr(self, k)) for k in "yzcxh")
        return ((y * 4 + z) * 2 + c, x * 4 + h)


def ring(at, by):
    return lax.rem(at + by + SIDE, SIDE)


class Sends:
    def __init__(self, sems):
        self.sems, self.count, self.kept = sems, 0, []

    def start(self, src, dst, recv_sem, device, when=None):
        slot = self.count
        self.count += 1

        def made():
            return pltpu.make_async_remote_copy(
                src_ref=src(), dst_ref=dst(), send_sem=self.sems.at[slot], recv_sem=recv_sem(),
                device_id=device, device_id_type=pl.DeviceIdType.MESH)

        if when is None:
            made().start()
        else:
            pl.when(when)(lambda: made().start())
        self.kept.append((made, when))

    def finish(self):
        for made, when in self.kept:
            if when is None:
                made().wait_send()
            else:
                pl.when(when)(lambda made=made: made().wait_send())


def arrived(view, sem, device):
    pltpu.make_async_remote_copy(
        src_ref=view, dst_ref=view, send_sem=sem, recv_sem=sem,
        device_id=device, device_id_type=pl.DeviceIdType.MESH).wait_recv()


def greet(devices):
    barrier = pltpu.get_barrier_semaphore()
    total = jnp.int32(0)
    for device, when in devices:
        def signal(device=device):
            pl.semaphore_signal(
                barrier, inc=1, device_id=device, device_id_type=pl.DeviceIdType.MESH)
        if when is None:
            signal()
            total = total + 1
        else:
            pl.when(when)(signal)
            total = total + when.astype(jnp.int32)
    pl.semaphore_wait(barrier, total)


def gather_partners(me):
    pairs = [(me.at(c=1 - me.c), None)]
    for by in (1, -1):
        pairs += [(me.at(y=ring(me.y, by)), None), (me.at(x=ring(me.x, by)), None),
                  (me.at(h=ring(me.h, by)), None)]
    pairs += [(me.at(z=me.z + 1), me.z < 3), (me.at(z=me.z - 1), me.z > 0)]
    return pairs


def gather_steps(me, sends, full, slab, pole_sems, twin_sems, slab_sems, weigh):
    rows, depth = full[0].shape[0] // 32, slab.shape[1] // 16
    twin = me.at(c=1 - me.c)

    def pole_view(half, y, z, c):
        at = ((y * 4 + z) * 2 + c) * rows
        return full[half].at[pl.ds(pl.multiple_of(at, rows), rows)]

    def send_pole(half, y, z, device, when=None):
        sends.start(lambda: pole_view(half, y, z, me.c), lambda: pole_view(half, y, z, me.c),
                    lambda: pole_sems.at[(y * 4 + z) * 2 + half], device, when)

    def send_twin(half, y, z, when=None):
        sends.start(lambda: pole_view(half, y, z, me.c), lambda: pole_view(half, y, z, me.c),
                    lambda: twin_sems.at[(y * 4 + z) * 2 + half], twin, when)

    def await_pole(half, y, z, when=None):
        def waits():
            arrived(pole_view(half, y, z, me.c), pole_sems.at[(y * 4 + z) * 2 + half], twin)
        waits() if when is None else pl.when(when)(waits)

    def slab_view(half, x, h):
        return slab.at[half, pl.ds(pl.multiple_of((x * 4 + h) * depth, depth), depth)]

    def send_slab(half, x, h, device):
        sends.start(lambda: slab_view(half, x, h), lambda: slab_view(half, x, h),
                    lambda: slab_sems.at[(x * 4 + h) * 2 + half], device)

    def await_slab(half, x, h):
        arrived(slab_view(half, x, h), slab_sems.at[(x * 4 + h) * 2 + half], twin)

    up, down = me.at(y=ring(me.y, 1)), me.at(y=ring(me.y, -1))
    east, west = me.at(x=ring(me.x, 1)), me.at(x=ring(me.x, -1))
    far, near = me.at(h=ring(me.h, 1)), me.at(h=ring(me.h, -1))
    right, left = me.at(z=me.z + 1), me.at(z=me.z - 1)

    def digest(y, by):
        def block(i, carry):
            z = me.z + (2 * i - 1) * by

            @pl.when((z >= 0) & (z <= 3))
            def _():
                for half in (0, 1):
                    arrived(pole_view(half, y, z, 1 - me.c), twin_sems.at[(y * 4 + z) * 2 + half], twin)
                weigh(y, z)
            return carry

        lax.fori_loop(0, 2 if by else 1, block, 0)

    def along_y(z, when=None):
        for half in (0, 1):
            send_pole(half, me.y, z, up, when)
            send_pole(half, me.y, z, down, when)

    def to_twin(y, z, when=None):
        for half in (0, 1):
            send_twin(half, y, z, when)

    def from_y(z, when=None):
        below, above = ring(me.y, -1), ring(me.y, 1)
        await_pole(0, below, z, when)
        send_pole(0, below, z, up, when)
        await_pole(1, above, z, when)
        send_pole(1, above, z, down, when)
        await_pole(1, below, z, when)
        await_pole(0, above, z, when)
        to_twin(below, z, when)
        to_twin(above, z, when)

    def from_opposite(z, when=None):
        across = ring(me.y, 2)
        for half in (0, 1):
            await_pole(half, across, z, when)
        to_twin(across, z, when)

    def from_z(by):
        for sign, onward, can in ((-1, right, me.z < 3), (1, left, me.z > 0)):
            z = me.z + sign * by
            there = (z >= 0) & (z <= 3)
            for half in (0, 1):
                await_pole(half, me.y, z, there)
                if by < 3:
                    send_pole(half, me.y, z, onward, there & can)
            along_y(z, there)
            to_twin(me.y, z, there)

    def sources(by):
        return [(z, (z >= 0) & (z <= 3)) for z in (me.z - by, me.z + by)]

    def along_x(h):
        for half in (0, 1):
            send_slab(half, me.x, h, east)
            send_slab(half, me.x, h, west)

    def from_x(h):
        behind, ahead = ring(me.x, -1), ring(me.x, 1)
        await_slab(0, behind, h)
        send_slab(0, behind, h, east)
        await_slab(1, ahead, h)
        send_slab(1, ahead, h, west)
        await_slab(1, behind, h)
        await_slab(0, ahead, h)

    def from_x_opposite(h):
        for half in (0, 1):
            await_slab(half, ring(me.x, 2), h)

    behind, ahead, across = ring(me.h, -1), ring(me.h, 1), ring(me.h, 2)

    def first():
        for half in (0, 1):
            send_pole(half, me.y, me.z, right, me.z < 3)
            send_pole(half, me.y, me.z, left, me.z > 0)
        along_y(me.z)
        to_twin(me.y, me.z)

    def slab_first():
        for half in (0, 1):
            send_slab(half, me.x, me.h, far)
            send_slab(half, me.x, me.h, near)

    def slab_second():
        await_slab(0, me.x, behind)
        send_slab(0, me.x, behind, far)
        await_slab(1, me.x, ahead)
        send_slab(1, me.x, ahead, near)
        await_slab(1, me.x, behind)
        await_slab(0, me.x, ahead)
        along_x(behind)
        along_x(ahead)

    def slab_third():
        for half in (0, 1):
            await_slab(half, me.x, across)
        along_x(across)

    below, above, opposite = ring(me.y, -1), ring(me.y, 1), ring(me.y, 2)

    def all_from_y(by):
        for z, there in sources(by):
            from_y(z, there)

    def all_from_opposite(by):
        for z, there in sources(by):
            from_opposite(z, there)

    def rest():
        from_z(1)
        along_x(me.h)
        digest(me.y, 0)
        from_z(2)
        slab_first()
        from_y(me.z)
        digest(me.y, 1)
        from_z(3)
        from_opposite(me.z)
        all_from_y(1)
        digest(below, 0)
        digest(above, 0)
        digest(opposite, 0)
        all_from_opposite(1)
        all_from_y(2)
        digest(me.y, 2)
        digest(below, 1)
        slab_second()
        digest(above, 1)
        from_x(me.h)
        all_from_opposite(2)
        all_from_y(3)
        digest(me.y, 3)
        digest(opposite, 1)
        slab_third()
        from_x(behind)
        from_x(ahead)
        digest(below, 2)
        from_x(across)
        digest(above, 2)
        for h in (me.h, behind, ahead, across):
            from_x_opposite(h)

    def last():
        digest(opposite, 2)
        digest(below, 3)
        all_from_opposite(3)
        digest(above, 3)
        digest(opposite, 3)

    return first, rest, last


def far_partners(me):
    pairs = [(me.at(x=ring(me.x, 2)), None), (me.at(h=ring(me.h, 2)), None), (me.at(y=ring(me.y, 2)), None)]
    for by in (1, 2, 3):
        pairs += [(me.at(y=ring(me.y, by), c=1 - me.c), None)]
        z = ring(me.z, by)
        pairs += [(me.at(z=z), jnp.abs(z - me.z) > 1)]
    return pairs


def reduce_steps(me, sends, product, part, out, out_twin, mine, twin, x_in, x_sum, y_in, y_sum, h_in, z_all, last, sems):
    other = me.at(c=1 - me.c)

    def await_(view, slot):
        arrived(view, sems.at[slot], other)

    def send(src, dst, slot, device):
        sends.start(lambda: src, lambda: dst, lambda: sems.at[slot], device)

    width = mine.shape[-1]
    theirs = pl.ds(pl.multiple_of((1 - me.c) * width, width), width)
    ours = pl.ds(pl.multiple_of(me.c * width, width), width)
    for by in (2, 1, 3, 0):
        x = ring(me.x, by)
        block = pl.ds(pl.multiple_of(x * 128, 128), 128)
        product(block)
        out_twin[x] = part[block, theirs].astype(jnp.bfloat16)
        send(out_twin.at[x], twin.at[x], by, other)
    for by in (2, 1, 3, 0):
        x = ring(me.x, by)
        block = pl.ds(pl.multiple_of(x * 128, 128), 128)
        await_(twin.at[x], by)
        summed = part[block, ours] + twin[x].astype(jnp.float32)
        if by:
            mine[x] = summed.astype(jnp.bfloat16)
            send(mine.at[x], x_in.at[by - 1], 4 + by - 1, me.at(x=x))
        else:
            x_sum[...] = summed.reshape(x_sum.shape)
    total = x_sum[...]
    for by in (3, 1, 2):
        await_(x_in.at[by - 1], 4 + by - 1)
        total = total + x_in[by - 1].astype(jnp.float32).reshape(x_sum.shape)
    x_sum[...] = total
    for by in (2, 1, 3):
        y = ring(me.y, by)
        send(x_sum.at[:, y], y_in.at[by - 1], 7 + by - 1, me.at(y=y))
    total = x_sum[:, me.y]
    for by in (3, 1, 2):
        await_(y_in.at[by - 1], 7 + by - 1)
        total = total + y_in[by - 1]
    y_sum[...] = total
    for by in (2, 1, 3):
        h = ring(me.h, by)
        send(y_sum.at[h], h_in.at[by - 1], 10 + by - 1, me.at(h=h))
    total = y_sum[me.h]
    for by in (3, 1, 2):
        await_(h_in.at[by - 1], 10 + by - 1)
        total = total + h_in[by - 1]
    z_all[me.z] = total
    for by in (2, 1, 3):
        z = ring(me.z, by)
        send(z_all.at[me.z], z_all.at[me.z], 13 + me.z, me.at(z=z))
    for by in (3, 1, 2):
        z = ring(me.z, by)
        await_(z_all.at[z], 13 + z)
    last[...] = (z_all[0] + z_all[1]) + (z_all[2] + z_all[3])
    rows = pl.ds(pl.multiple_of(me.y * 8, 8), 8)
    slot = 17 + me.y * 2 + me.c
    for by in (2, 1, 3):
        y = ring(me.y, by)
        send(last, out.at[rows, ours], slot, me.at(y=y))
        send(last, out.at[rows, ours], slot, me.at(y=y, c=1 - me.c))
    send(last, out.at[rows, ours], slot, other)
    out[rows, ours] = last[...]
    for by in (0, 1, 2, 3):
        y = ring(me.y, by)
        there = pl.ds(pl.multiple_of(y * 8, 8), 8)
        if by:
            await_(out.at[there, ours], 17 + y * 2 + me.c)
        await_(out.at[there, theirs], 17 + y * 2 + 1 - me.c)


def reduce_scratch():
    f32, bf16 = jnp.float32, jnp.bfloat16
    return [
        pltpu.VMEM((4, 128, 256), bf16), pltpu.VMEM((4, 128, 256), bf16),
        pltpu.VMEM((4, 128, 256), bf16), pltpu.VMEM((3, 128, 256), bf16),
        pltpu.VMEM((4, 4, 8, 256), f32),
        pltpu.VMEM((3, 4, 8, 256), f32), pltpu.VMEM((4, 8, 256), f32),
        pltpu.VMEM((3, 8, 256), f32), pltpu.VMEM((4, 8, 256), f32),
        pltpu.VMEM((8, 256), f32), pltpu.SemaphoreType.DMA((25,)),
    ]


def chosen_band(order, mags, slot, occupied):
    lanes = lax.broadcasted_iota(jnp.int32, order.shape, 1)
    band = jnp.sum(jnp.where(lanes == slot, order, 0), axis=1, keepdims=True)
    magnitude = jnp.sum(jnp.where(lanes == band, mags, 0.0), axis=1, keepdims=True)
    return magnitude, jnp.where(band < occupied, 1.0, -1.0).astype(jnp.float32)


def whole_kernel(normalizer, elems_hbm, res_hbm, pole_hbm, index, order, mags, out,
                 elems, split, poles, ress, slab, slab_n, weights, mixed, part,
                 send_sems, pole_sems, twin_sems, slab_sems, own_sems, *reduce_refs):
    me = Place()
    rows, width = pole_hbm.shape
    states = elems.shape[0]
    depth = index.shape[1]
    pool, col = lax.axis_index("pool"), lax.axis_index("col")
    bf16, f32 = jnp.bfloat16, jnp.float32
    at = pl.ds(pl.multiple_of(pool * rows, rows), rows)
    loads = [
        pltpu.make_async_copy(pole_hbm, poles.at[at], own_sems.at[0]),
        pltpu.make_async_copy(res_hbm, ress.at[at], own_sems.at[1]),
        pltpu.make_async_copy(elems_hbm, elems, own_sems.at[2]),
    ]
    for load in loads:
        load.start()
    greet(gather_partners(me) + far_partners(me))
    sends = Sends(send_sems)
    bands = [chosen_band(order[...], mags[...], pool * 2 + j, order.shape[1] // 4) for j in (0, 1)]

    def weigh(y, z):
        first_row = pl.multiple_of((y * 4 + z) * 2 * rows, 2 * rows)

        def chunk(k, carry):
            block = pl.ds(first_row, 2 * rows)
            lanes = pl.ds(pl.multiple_of(k * 256, 256), 256)
            pole, res = poles[block, lanes].astype(f32), ress[block, lanes].astype(f32)
            for j, (magnitude, parity) in enumerate(bands):
                gap = parity * (pole + magnitude)
                scaled = res * gap / (gap * gap + broadening * broadening)
                weights[j, :, lanes] = scaled.astype(bf16)
            return carry

        lax.fori_loop(0, width // 256, chunk, 0)
        for j in (0, 1):
            mixed[j, pl.ds(first_row, 2 * rows)] = lax.dot_general(
                weights[j], split[j], (((1,), (1,)), ((), ())), preferred_element_type=f32).astype(bf16)

    first, rest, last = gather_steps(
        me, sends, (poles, ress), slab, pole_sems, twin_sems, slab_sems, weigh)
    loads[0].wait()
    loads[1].wait()
    first()

    loads[2].wait()
    to = lax.broadcasted_iota(jnp.int32, (256, 256), 0)
    came = lax.broadcasted_iota(jnp.int32, (256, 256), 1)
    swap = (came == (to % 128) * 2 + to // 128).astype(bf16)

    def part_by_slot(i, carry):
        n = pl.ds(pl.multiple_of(i * 128, 128), 128)
        pairs = elems[n].reshape(256, width)
        sorted_rows = jnp.dot(swap, pairs, preferred_element_type=f32).astype(bf16)
        split[0, n] = sorted_rows[:128]
        split[1, n] = sorted_rows[128:]
        return carry

    lax.fori_loop(0, states // 128, part_by_slot, 0)
    diagonal = lax.broadcasted_iota(jnp.int32, (depth, depth), 0) == lax.broadcasted_iota(
        jnp.int32, (depth, depth), 1)
    local = jnp.sum(jnp.where(diagonal, index[...] - col * width, 0), axis=1, keepdims=True)
    chosen = (lax.broadcasted_iota(jnp.int32, (depth, width), 1) == local).astype(bf16)
    own_slab = pl.ds(pl.multiple_of(col * depth, depth), depth)
    for j in (0, 1):
        slab[j, own_slab] = lax.dot_general(
            chosen, split[j], (((1,), (1,)), ((), ())), preferred_element_type=f32).astype(bf16)

    rest()
    for j in (0, 1):
        slab_n[j] = slab[j].T
    last()

    def product(block):
        for j in (0, 1):
            term = jnp.dot(slab_n[j, block], mixed[j], preferred_element_type=f32) * normalizer
            part[block] = term if j == 0 else part[block] + term

    reduce_steps(me, sends, product, part, out, *reduce_refs)
    sends.finish()


def on_device(matrix_elems, residue, pole_freq, slab_index, band_order, band_mag):
    states, members, width = matrix_elems.shape
    rows, slab_rows = residue.shape[0], residue.shape[0] * 32
    bands = band_order.shape[0]
    normalizer = float(1.0 / np.sqrt(np.float32(bands * slab_rows * width * 16)))
    dma, vmem, anywhere = pltpu.SemaphoreType.DMA, pltpu.VMEM, pl.BlockSpec(memory_space=pl.ANY)
    whole = pl.BlockSpec(memory_space=pltpu.VMEM)
    bf16 = jnp.bfloat16
    return pl.pallas_call(
        functools.partial(whole_kernel, normalizer),
        out_shape=jax.ShapeDtypeStruct((states // 16, states), jnp.float32),
        in_specs=[anywhere] * 3 + [whole] * 3,
        out_specs=whole,
        scratch_shapes=[
            vmem((states, members, width), bf16), vmem((members, states, width), bf16),
            vmem((slab_rows, width), bf16), vmem((slab_rows, width), bf16),
            vmem((members, slab_rows, states), bf16), vmem((members, states, slab_rows), bf16),
            vmem((members, 2 * rows, width), bf16), vmem((members, slab_rows, states), bf16),
            vmem((states, states), jnp.float32),
            dma((SENDS,)), dma((32,)), dma((32,)), dma((32,)), dma((3,)),
        ] + reduce_scratch(),
        compiler_params=pltpu.CompilerParams(
            collective_id=0, has_side_effects=True, vmem_limit_bytes=60 * 2**20),
    )(matrix_elems, residue, pole_freq, slab_index[None], band_order[None], band_mag[None])


def solution(mesh):
    placed = (P(None, "pool", "col"), P("pool", "col"), P("pool", "col"), P("col"), P(), P())
    return jax.shard_map(
        on_device, mesh=mesh, in_specs=placed, out_specs=P("col", None), check_vma=False
    )
```

```python
import functools

import jax
import jax.numpy as jnp
import numpy as np
from jax import lax
from jax.experimental import pallas as pl
from jax.experimental.pallas import tpu as pltpu
from jax.sharding import PartitionSpec as P

broadening = 0.25
SIDE = 4
SENDS = 200


class Place:
    def __init__(self):
        pool, col = lax.axis_index("pool"), lax.axis_index("col")
        self.y, self.z, self.c = pool // 8, (pool // 2) % 4, pool % 2
        self.x, self.h = col // 4, col % 4

    def at(self, **moved):
        y, z, c, x, h = (moved.get(k, getattr(self, k)) for k in "yzcxh")
        return ((y * 4 + z) * 2 + c, x * 4 + h)


def ring(at, by):
    return lax.rem(at + by + SIDE, SIDE)


class Sends:
    def __init__(self, sems):
        self.sems, self.count, self.kept = sems, 0, []

    def start(self, src, dst, recv_sem, device, when=None):
        slot = self.count
        self.count += 1

        def made():
            return pltpu.make_async_remote_copy(
                src_ref=src(), dst_ref=dst(), send_sem=self.sems.at[slot], recv_sem=recv_sem(),
                device_id=device, device_id_type=pl.DeviceIdType.MESH)

        if when is None:
            made().start()
        else:
            pl.when(when)(lambda: made().start())
        self.kept.append((made, when))

    def finish(self):
        for made, when in self.kept:
            if when is None:
                made().wait_send()
            else:
                pl.when(when)(lambda made=made: made().wait_send())


def arrived(view, sem, device):
    pltpu.make_async_remote_copy(
        src_ref=view, dst_ref=view, send_sem=sem, recv_sem=sem,
        device_id=device, device_id_type=pl.DeviceIdType.MESH).wait_recv()


def greet(devices):
    barrier = pltpu.get_barrier_semaphore()
    total = jnp.int32(0)
    for device, when in devices:
        def signal(device=device):
            pl.semaphore_signal(
                barrier, inc=1, device_id=device, device_id_type=pl.DeviceIdType.MESH)
        if when is None:
            signal()
            total = total + 1
        else:
            pl.when(when)(signal)
            total = total + when.astype(jnp.int32)
    pl.semaphore_wait(barrier, total)


def gather_partners(me):
    pairs = [(me.at(c=1 - me.c), None)]
    for by in (1, -1):
        pairs += [(me.at(y=ring(me.y, by)), None), (me.at(x=ring(me.x, by)), None),
                  (me.at(h=ring(me.h, by)), None)]
    pairs += [(me.at(z=me.z + 1), me.z < 3), (me.at(z=me.z - 1), me.z > 0)]
    return pairs


def gather_steps(me, sends, full, slab, pole_sems, twin_sems, slab_sems, weigh, row_products):
    rows, depth = full[0].shape[0] // 32, slab.shape[1] // 16
    twin = me.at(c=1 - me.c)

    def pole_view(half, y, z, c):
        at = ((y * 4 + z) * 2 + c) * rows
        return full[half].at[pl.ds(pl.multiple_of(at, rows), rows)]

    def send_pole(half, y, z, device, when=None):
        sends.start(lambda: pole_view(half, y, z, me.c), lambda: pole_view(half, y, z, me.c),
                    lambda: pole_sems.at[(y * 4 + z) * 2 + half], device, when)

    def send_twin(half, y, z, when=None):
        sends.start(lambda: pole_view(half, y, z, me.c), lambda: pole_view(half, y, z, me.c),
                    lambda: twin_sems.at[(y * 4 + z) * 2 + half], twin, when)

    def await_pole(half, y, z, when=None):
        def waits():
            arrived(pole_view(half, y, z, me.c), pole_sems.at[(y * 4 + z) * 2 + half], twin)
        waits() if when is None else pl.when(when)(waits)

    def slab_view(half, x, h):
        return slab.at[half, pl.ds(pl.multiple_of((x * 4 + h) * depth, depth), depth)]

    def send_slab(half, x, h, device):
        sends.start(lambda: slab_view(half, x, h), lambda: slab_view(half, x, h),
                    lambda: slab_sems.at[(x * 4 + h) * 2 + half], device)

    def await_slab(half, x, h):
        arrived(slab_view(half, x, h), slab_sems.at[(x * 4 + h) * 2 + half], twin)

    up, down = me.at(y=ring(me.y, 1)), me.at(y=ring(me.y, -1))
    east, west = me.at(x=ring(me.x, 1)), me.at(x=ring(me.x, -1))
    far, near = me.at(h=ring(me.h, 1)), me.at(h=ring(me.h, -1))
    right, left = me.at(z=me.z + 1), me.at(z=me.z - 1)

    def digest(y, by):
        def block(i, carry):
            z = me.z + (2 * i - 1) * by

            @pl.when((z >= 0) & (z <= 3))
            def _():
                for half in (0, 1):
                    arrived(pole_view(half, y, z, 1 - me.c), twin_sems.at[(y * 4 + z) * 2 + half], twin)
                weigh(y, z)
            return carry

        lax.fori_loop(0, 2 if by else 1, block, 0)

    def along_y(z, when=None):
        for half in (0, 1):
            send_pole(half, me.y, z, up, when)
            send_pole(half, me.y, z, down, when)

    def to_twin(y, z, when=None):
        for half in (0, 1):
            send_twin(half, y, z, when)

    def from_y(z, when=None):
        below, above = ring(me.y, -1), ring(me.y, 1)
        await_pole(0, below, z, when)
        send_pole(0, below, z, up, when)
        await_pole(1, above, z, when)
        send_pole(1, above, z, down, when)
        await_pole(1, below, z, when)
        await_pole(0, above, z, when)
        to_twin(below, z, when)
        to_twin(above, z, when)

    def from_opposite(z, when=None):
        across = ring(me.y, 2)
        for half in (0, 1):
            await_pole(half, across, z, when)
        to_twin(across, z, when)

    def from_z(by):
        for sign, onward, can in ((-1, right, me.z < 3), (1, left, me.z > 0)):
            z = me.z + sign * by
            there = (z >= 0) & (z <= 3)
            for half in (0, 1):
                await_pole(half, me.y, z, there)
                if by < 3:
                    send_pole(half, me.y, z, onward, there & can)
            along_y(z, there)
            to_twin(me.y, z, there)

    def sources(by):
        return [(z, (z >= 0) & (z <= 3)) for z in (me.z - by, me.z + by)]

    def along_x(h):
        for half in (0, 1):
            send_slab(half, me.x, h, east)
            send_slab(half, me.x, h, west)

    def from_x(h):
        behind, ahead = ring(me.x, -1), ring(me.x, 1)
        await_slab(0, behind, h)
        send_slab(0, behind, h, east)
        await_slab(1, ahead, h)
        send_slab(1, ahead, h, west)
        await_slab(1, behind, h)
        await_slab(0, ahead, h)

    def from_x_opposite(h):
        for half in (0, 1):
            await_slab(half, ring(me.x, 2), h)

    behind, ahead, across = ring(me.h, -1), ring(me.h, 1), ring(me.h, 2)

    def first():
        for half in (0, 1):
            send_pole(half, me.y, me.z, right, me.z < 3)
            send_pole(half, me.y, me.z, left, me.z > 0)
        along_y(me.z)
        to_twin(me.y, me.z)

    def slab_first():
        for half in (0, 1):
            send_slab(half, me.x, me.h, far)
            send_slab(half, me.x, me.h, near)
        along_x(me.h)

    def slab_second():
        await_slab(0, me.x, behind)
        send_slab(0, me.x, behind, far)
        await_slab(1, me.x, ahead)
        send_slab(1, me.x, ahead, near)
        await_slab(1, me.x, behind)
        await_slab(0, me.x, ahead)
        along_x(behind)
        along_x(ahead)

    def slab_third():
        for half in (0, 1):
            await_slab(half, me.x, across)
        along_x(across)

    below, above, opposite = ring(me.y, -1), ring(me.y, 1), ring(me.y, 2)

    def all_from_y(by):
        for z, there in sources(by):
            from_y(z, there)

    def all_from_opposite(by):
        for z, there in sources(by):
            from_opposite(z, there)

    def rest():
        from_z(1)
        slab_first()
        digest(me.y, 0)
        from_z(2)
        from_y(me.z)
        digest(me.y, 1)
        from_z(3)
        all_from_y(1)
        from_opposite(me.z)
        slab_second()
        digest(below, 0)
        digest(above, 0)
        all_from_y(2)
        from_x(me.h)
        digest(opposite, 0)
        digest(me.y, 2)
        all_from_opposite(1)
        slab_third()
        from_x(behind)
        from_x(ahead)
        digest(below, 1)
        digest(above, 1)
        digest(me.y, 3)
        all_from_y(3)
        all_from_opposite(2)
        from_x(across)
        digest(opposite, 1)
        digest(below, 2)
        digest(above, 2)
        row_products(me.y)
        for h in (me.h, behind, ahead, across):
            from_x_opposite(h)

    def last():
        digest(below, 3)
        digest(above, 3)
        row_products(below)
        all_from_opposite(3)
        row_products(above)
        digest(opposite, 2)
        digest(opposite, 3)
        row_products(opposite)

    return first, rest, last


def far_partners(me):
    pairs = [(me.at(x=ring(me.x, 2)), None), (me.at(h=ring(me.h, 2)), None), (me.at(y=ring(me.y, 2)), None)]
    for by in (1, 2, 3):
        pairs += [(me.at(y=ring(me.y, by), c=1 - me.c), None)]
        z = ring(me.z, by)
        pairs += [(me.at(z=z), jnp.abs(z - me.z) > 1)]
    return pairs


def reduce_steps(me, sends, product, part, out, out_twin, mine, twin, x_in, x_sum, y_in, y_sum, h_in, z_all, last, sems):
    other = me.at(c=1 - me.c)

    def await_(view, slot):
        arrived(view, sems.at[slot], other)

    def send(src, dst, slot, device):
        sends.start(lambda: src, lambda: dst, lambda: sems.at[slot], device)

    width = mine.shape[-1]
    theirs = pl.ds(pl.multiple_of((1 - me.c) * width, width), width)
    ours = pl.ds(pl.multiple_of(me.c * width, width), width)
    for by in (2, 1, 3, 0):
        x = ring(me.x, by)
        block = pl.ds(pl.multiple_of(x * 128, 128), 128)
        product(block)
        out_twin[x] = part[block, theirs].astype(jnp.bfloat16)
        send(out_twin.at[x], twin.at[x], by, other)
    for by in (2, 1, 3, 0):
        x = ring(me.x, by)
        block = pl.ds(pl.multiple_of(x * 128, 128), 128)
        await_(twin.at[x], by)
        summed = part[block, ours] + twin[x].astype(jnp.float32)
        if by:
            mine[x] = summed.astype(jnp.bfloat16)
            send(mine.at[x], x_in.at[by - 1], 4 + by - 1, me.at(x=x))
        else:
            x_sum[...] = summed.reshape(x_sum.shape)
    total = x_sum[...]
    for by in (3, 1, 2):
        await_(x_in.at[by - 1], 4 + by - 1)
        total = total + x_in[by - 1].astype(jnp.float32).reshape(x_sum.shape)
    x_sum[...] = total
    for by in (2, 1, 3):
        y = ring(me.y, by)
        send(x_sum.at[:, y], y_in.at[by - 1], 7 + by - 1, me.at(y=y))
    total = x_sum[:, me.y]
    for by in (3, 1, 2):
        await_(y_in.at[by - 1], 7 + by - 1)
        total = total + y_in[by - 1]
    y_sum[...] = total
    for by in (2, 1, 3):
        h = ring(me.h, by)
        send(y_sum.at[h], h_in.at[by - 1], 10 + by - 1, me.at(h=h))
    total = y_sum[me.h]
    for by in (3, 1, 2):
        await_(h_in.at[by - 1], 10 + by - 1)
        total = total + h_in[by - 1]
    z_all[me.z] = total
    for by in (2, 1, 3):
        z = ring(me.z, by)
        send(z_all.at[me.z], z_all.at[me.z], 13 + me.z, me.at(z=z))
    for by in (3, 1, 2):
        z = ring(me.z, by)
        await_(z_all.at[z], 13 + z)
    last[...] = (z_all[0] + z_all[1]) + (z_all[2] + z_all[3])
    rows = pl.ds(pl.multiple_of(me.y * 8, 8), 8)
    slot = 17 + me.y * 2 + me.c
    for by in (2, 1, 3):
        y = ring(me.y, by)
        send(last, out.at[rows, ours], slot, me.at(y=y))
        send(last, out.at[rows, ours], slot, me.at(y=y, c=1 - me.c))
    send(last, out.at[rows, ours], slot, other)
    out[rows, ours] = last[...]
    for by in (0, 1, 2, 3):
        y = ring(me.y, by)
        there = pl.ds(pl.multiple_of(y * 8, 8), 8)
        if by:
            await_(out.at[there, ours], 17 + y * 2 + me.c)
        await_(out.at[there, theirs], 17 + y * 2 + 1 - me.c)


def reduce_scratch():
    f32, bf16 = jnp.float32, jnp.bfloat16
    return [
        pltpu.VMEM((4, 128, 256), bf16), pltpu.VMEM((4, 128, 256), bf16),
        pltpu.VMEM((4, 128, 256), bf16), pltpu.VMEM((3, 128, 256), bf16),
        pltpu.VMEM((4, 4, 8, 256), f32),
        pltpu.VMEM((3, 4, 8, 256), f32), pltpu.VMEM((4, 8, 256), f32),
        pltpu.VMEM((3, 8, 256), f32), pltpu.VMEM((4, 8, 256), f32),
        pltpu.VMEM((8, 256), f32), pltpu.SemaphoreType.DMA((25,)),
    ]


def chosen_band(order, mags, slot, occupied):
    lanes = lax.broadcasted_iota(jnp.int32, order.shape, 1)
    band = jnp.sum(jnp.where(lanes == slot, order, 0), axis=1, keepdims=True)
    magnitude = jnp.sum(jnp.where(lanes == band, mags, 0.0), axis=1, keepdims=True)
    return magnitude, jnp.where(band < occupied, 1.0, -1.0).astype(jnp.float32)


def whole_kernel(normalizer, elems_hbm, res_hbm, pole_hbm, index, order, mags, out,
                 elems, split, poles, ress, slab, slab_n, weights, mixed, part,
                 send_sems, pole_sems, twin_sems, slab_sems, own_sems, *reduce_refs):
    me = Place()
    rows, width = pole_hbm.shape
    states = elems.shape[0]
    depth = index.shape[1]
    pool, col = lax.axis_index("pool"), lax.axis_index("col")
    bf16, f32 = jnp.bfloat16, jnp.float32
    at = pl.ds(pl.multiple_of(pool * rows, rows), rows)
    loads = [
        pltpu.make_async_copy(pole_hbm, poles.at[at], own_sems.at[0]),
        pltpu.make_async_copy(res_hbm, ress.at[at], own_sems.at[1]),
        pltpu.make_async_copy(elems_hbm, elems, own_sems.at[2]),
    ]
    for load in loads:
        load.start()
    greet(gather_partners(me) + far_partners(me))
    sends = Sends(send_sems)
    bands = [chosen_band(order[...], mags[...], pool * 2 + j, order.shape[1] // 4) for j in (0, 1)]

    def weigh(y, z):
        first_row = pl.multiple_of((y * 4 + z) * 2 * rows, 2 * rows)

        def chunk(k, carry):
            block = pl.ds(first_row, 2 * rows)
            lanes = pl.ds(pl.multiple_of(k * 256, 256), 256)
            pole, res = poles[block, lanes].astype(f32), ress[block, lanes].astype(f32)
            for j, (magnitude, parity) in enumerate(bands):
                gap = parity * (pole + magnitude)
                scaled = res * gap / (gap * gap + broadening * broadening)
                weights[j, block, lanes] = scaled.astype(bf16)
            return carry

        lax.fori_loop(0, width // 256, chunk, 0)

    def row_products(y):
        block = pl.ds(pl.multiple_of(y * 8 * rows, 8 * rows), 8 * rows)
        for j in (0, 1):
            mixed[j, block] = lax.dot_general(
                weights[j, block], split[j], (((1,), (1,)), ((), ())), preferred_element_type=f32).astype(bf16)

    first, rest, last = gather_steps(
        me, sends, (poles, ress), slab, pole_sems, twin_sems, slab_sems, weigh, row_products)
    loads[0].wait()
    loads[1].wait()
    first()

    loads[2].wait()
    to = lax.broadcasted_iota(jnp.int32, (256, 256), 0)
    came = lax.broadcasted_iota(jnp.int32, (256, 256), 1)
    swap = (came == (to % 128) * 2 + to // 128).astype(bf16)

    def part_by_slot(i, carry):
        n = pl.ds(pl.multiple_of(i * 128, 128), 128)
        pairs = elems[n].reshape(256, width)
        sorted_rows = jnp.dot(swap, pairs, preferred_element_type=f32).astype(bf16)
        split[0, n] = sorted_rows[:128]
        split[1, n] = sorted_rows[128:]
        return carry

    lax.fori_loop(0, states // 128, part_by_slot, 0)
    diagonal = lax.broadcasted_iota(jnp.int32, (depth, depth), 0) == lax.broadcasted_iota(
        jnp.int32, (depth, depth), 1)
    local = jnp.sum(jnp.where(diagonal, index[...] - col * width, 0), axis=1, keepdims=True)
    chosen = (lax.broadcasted_iota(jnp.int32, (depth, width), 1) == local).astype(bf16)
    own_slab = pl.ds(pl.multiple_of(col * depth, depth), depth)
    for j in (0, 1):
        slab[j, own_slab] = lax.dot_general(
            chosen, split[j], (((1,), (1,)), ((), ())), preferred_element_type=f32).astype(bf16)

    rest()
    for j in (0, 1):
        slab_n[j] = slab[j].T
    last()

    def product(block):
        for j in (0, 1):
            term = jnp.dot(slab_n[j, block], mixed[j], preferred_element_type=f32) * normalizer
            part[block] = term if j == 0 else part[block] + term

    reduce_steps(me, sends, product, part, out, *reduce_refs)
    sends.finish()


def on_device(matrix_elems, residue, pole_freq, slab_index, band_order, band_mag):
    states, members, width = matrix_elems.shape
    rows, slab_rows = residue.shape[0], residue.shape[0] * 32
    bands = band_order.shape[0]
    normalizer = float(1.0 / np.sqrt(np.float32(bands * slab_rows * width * 16)))
    dma, vmem, anywhere = pltpu.SemaphoreType.DMA, pltpu.VMEM, pl.BlockSpec(memory_space=pl.ANY)
    whole = pl.BlockSpec(memory_space=pltpu.VMEM)
    bf16 = jnp.bfloat16
    return pl.pallas_call(
        functools.partial(whole_kernel, normalizer),
        out_shape=jax.ShapeDtypeStruct((states // 16, states), jnp.float32),
        in_specs=[anywhere] * 3 + [whole] * 3,
        out_specs=whole,
        scratch_shapes=[
            vmem((states, members, width), bf16), vmem((members, states, width), bf16),
            vmem((slab_rows, width), bf16), vmem((slab_rows, width), bf16),
            vmem((members, slab_rows, states), bf16), vmem((members, states, slab_rows), bf16),
            vmem((members, slab_rows, width), bf16), vmem((members, slab_rows, states), bf16),
            vmem((states, states), jnp.float32),
            dma((SENDS,)), dma((32,)), dma((32,)), dma((32,)), dma((3,)),
        ] + reduce_scratch(),
        compiler_params=pltpu.CompilerParams(
            collective_id=0, has_side_effects=True, vmem_limit_bytes=60 * 2**20),
    )(matrix_elems, residue, pole_freq, slab_index[None], band_order[None], band_mag[None])


def solution(mesh):
    placed = (P(None, "pool", "col"), P("pool", "col"), P("pool", "col"), P("col"), P(), P())
    return jax.shard_map(
        on_device, mesh=mesh, in_specs=placed, out_specs=P("col", None), check_vma=False
    )
```
